32 devices in a mesh: group: 2 (over y), tile: 4 (over z), head: 4 (over x, core).
Axes of the slice: x: 2, y: 2, z: 4, core: 2. Of those that a mesh axis runs over, the one named last changes fastest.
Arguments:
- latent: bfloat16 [32, 6, 32, 3072], P(('group', 'tile'), None, None, 'head'), parts along dimension 0, may hold values from -6 to 6
- text_tokens: bfloat16 [512, 3072], P('group'), parts along dimension 0, may hold values from -6 to 6
- mod_shift: float32 [3072], replicated, may hold values from -3 to 3
- mod_scale: float32 [3072], replicated, may hold values from -2.5 to 2.5
- mod_gate: float32 [3072], replicated, may hold values from 0.5 to 2
- project_in: bfloat16 [3072, 3, 3072], P(None, None, 'head')
- project_out: bfloat16 [3072, 3072], P('head'), may hold values from -0.109375 to 0.109375
- q_gain: float32 [128], replicated, may hold values from 0.7 to 7
- k_gain: float32 [128], replicated, may hold values from 0.7 to 7
- pattern: int32 [8, 4], P('tile'), may hold values from 0 to 5, as said below
- tile_rows: int32 [16], P('group'), parts along dimension 0, may hold values from 96 to 384, as said below
- text_mask: int32 [512], P('group'), parts along dimension 0, may hold values from 0 to 1, as said below
Outputs:
- update: bfloat16 [32, 6, 32, 3072], P(('group', 'head'), None, 'tile'), parts along dimension 0
- text_update: bfloat16 [512, 3072], P(('group', 'head')), parts along dimension 0
The draws below stay inside these ranges and needn't reach their ends.
There are 2 independent parts, one for each index of `group`. The reference program is written for one: setup_inputs(seed, part) draws one part's arguments, and reference() takes and returns one part's arrays. A program takes and returns all parts, laid end to end along the dimension named above; an argument that names none is the same for every part. Nothing has to cross between parts.
Inputs may be any that keep to these rules, and one draw needn't show every extreme that they name: `pattern`: entries of a row are distinct, the first is the query tile itself (s = 2 + its index in its band), and none names a band outside the grid. `tile_rows`: tiles of the last column band hold from 96 to 384 real tokens; every other tile holds 384. `text_mask`: the ones form a prefix of at least 32 positions.
All inputs are finite; a program needn't handle non-finite values.
Results may differ from the reference program's by a relative error of at most 0.015.
The reference program's roundings to bfloat16 on the way count: a program that leaves them out, or rounds other values in their place, can miss the bound.
Values may be sent and summed in bfloat16 or wider, within the bound.
No kernel may reach another device: no remote copies, remote signals or barrier semaphores. Data moves between devices by JAX's collectives and lax.ppermute only.
A program may use at most 128 MiB of HBM per device.

```python
import math
import jax
import jax.numpy as jnp
from jax import lax

D = 3072
HEADS = 24
HD = 128
F = 16
H = 6
TF = 8
TH = 6
TW = 8
NWIN = 4
TEXT = 256
W = 32
N_HEAD = 4


def draw_project_in(key, part):
    base = jax.random.normal(jax.random.fold_in(key, 11), (D, 3, HEADS * HD), jnp.float32) / math.sqrt(D)
    return base.astype(jnp.bfloat16)


def draw_q_gain(key, part):
    return jax.random.uniform(jax.random.fold_in(key, 21), (HD,), jnp.float32, 0.7, 1.6)


def draw_k_gain(key, part):
    return jax.random.uniform(jax.random.fold_in(key, 22), (HD,), jnp.float32, 0.7, 1.6)


def draw_pattern(key, part):
    band_count = W // TW
    per_device = F // TF * (H // TH)
    tile_total = per_device * band_count
    tile_ids = jnp.arange(tile_total, dtype=jnp.int32)
    owners = tile_ids // per_device
    local_ids = tile_ids % per_device
    slot_ids = jnp.arange(3 * per_device, dtype=jnp.int32)
    targets = owners[:, None] + slot_ids[None, :] // per_device - 1
    inside = (targets >= 0) & (targets < band_count)
    itself = slot_ids[None, :] == (per_device + local_ids)[:, None]
    ranking = jax.random.randint(jax.random.fold_in(key, 31), (tile_total, 3 * per_device), 0, 1 << 20) * 64 + slot_ids[None, :]
    ranking = jnp.where(inside & jnp.logical_not(itself), ranking, -1)
    picked_scores, picked = lax.top_k(ranking, NWIN - 1)
    return jnp.concatenate([(per_device + local_ids)[:, None], picked.astype(jnp.int32)], axis=1).astype(jnp.int32)


def draw_tile_rows(key, part):
    band_count = W // TW
    per_device = F // TF * (H // TH)
    tile_size = TF * TH * TW
    tile_ids = jnp.arange(per_device * band_count, dtype=jnp.int32)
    shorter = jax.random.randint(jax.random.fold_in(key, 41), (per_device * band_count,), tile_size // 4, tile_size + 1)
    return jnp.where(tile_ids // per_device == band_count - 1, shorter, tile_size).astype(jnp.int32)


def draw_text_mask(key, part):
    prompt_length = jax.random.randint(jax.random.fold_in(key, 51), (), TEXT // 8, TEXT + 1)
    return (jnp.arange(TEXT, dtype=jnp.int32) < prompt_length).astype(jnp.int32)


def block_levels(stream_key, dims, split, low, largest):
    gain = 1.0
    for dim, parts in split:
        draws = jax.random.uniform(jax.random.fold_in(jax.random.fold_in(stream_key, 6), dim), (parts,), jnp.float32, low / len(split), largest / len(split))
        gain = gain * jnp.repeat(jnp.exp(draws), dims[dim] // parts).reshape((-1,) + (1,) * (len(dims) - 1 - dim))
    return gain


def gaussian(stream_key, shape, width, bound, split=(), kind=jnp.bfloat16):
    level = block_levels(stream_key, shape, split, -0.22, 0.18) if split else 1.0
    result = jax.random.normal(stream_key, shape, jnp.float32) * width * level
    return jnp.minimum(jnp.maximum(result, -bound), bound).astype(kind)


def setup_inputs(seed: int = 0, part: int = 0) -> dict:
    seeds = jax.random.split(jax.random.key(seed), 13)
    own_keys = jax.random.split(jax.random.fold_in(seeds[12], part), 13)
    latent = gaussian(own_keys[0], (F, H, W, D), 1.0, 6.0, ((0, 4), (3, 4)))
    text_tokens = gaussian(own_keys[1], (TEXT, D), 1.0, 6.0)
    mod_shift = gaussian(seeds[2], (D,), 0.5, 3.0, (), jnp.float32)
    mod_scale = gaussian(seeds[3], (D,), 0.5, 2.5, (), jnp.float32)
    mod_gate = jnp.clip(jax.random.uniform(seeds[4], (D,), jnp.float32, 0.5, 2.0), 0.5, 2.0)
    project_in = draw_project_in(jax.random.fold_in(seeds[12], 71), part)
    project_out = gaussian(seeds[6], (HEADS * HD, D), (HEADS * HD) ** -0.5, 0.109375, ((0, 4),))
    q_gain = draw_q_gain(jax.random.fold_in(seeds[12], 71), part)
    k_gain = draw_k_gain(jax.random.fold_in(seeds[12], 71), part)
    pattern = draw_pattern(jax.random.fold_in(seeds[12], 71), part)
    tile_rows = draw_tile_rows(jax.random.fold_in(jax.random.fold_in(seeds[12], part), 71), part)
    text_mask = draw_text_mask(jax.random.fold_in(jax.random.fold_in(seeds[12], part), 71), part)
    return dict(latent=latent, text_tokens=text_tokens, mod_shift=mod_shift, mod_scale=mod_scale, mod_gate=mod_gate, project_in=project_in, project_out=project_out, q_gain=q_gain, k_gain=k_gain, pattern=pattern, tile_rows=tile_rows, text_mask=text_mask)


EPSILON = 1e-06

def modulate(values, mod_shift, mod_scale):
    widened = values.astype(jnp.float32)
    center = lax.optimization_barrier(jnp.mean(widened, axis=-1, keepdims=True))
    offset = widened - center
    variance = lax.optimization_barrier(jnp.mean(offset * offset, axis=-1, keepdims=True))
    return (offset * lax.rsqrt(variance + EPSILON) * (1.0 + mod_scale) + mod_shift).astype(jnp.bfloat16)

def rms_gain(values, gains):
    square = lax.optimization_barrier(jnp.mean(values * values, axis=-1, keepdims=True))
    return (values * lax.rsqrt(square + EPSILON) * gains).astype(jnp.bfloat16)

def attend(queries, key_rows, value_rows, usable):
    scores = jnp.einsum('qhd,khd->hqk', queries.astype(jnp.float32), key_rows.astype(jnp.float32), precision=lax.Precision.HIGHEST) / math.sqrt(HD)
    scores = jnp.where(usable[None, None, :], scores, -jnp.inf)
    highest = lax.optimization_barrier(jnp.max(scores, axis=-1, keepdims=True))
    weights = jnp.exp(scores - highest)
    sums_row = lax.optimization_barrier(jnp.sum(weights, axis=-1))
    rounded = lax.optimization_barrier(weights.astype(jnp.bfloat16)).astype(jnp.float32)
    blended = jnp.einsum('hqk,khd->qhd', rounded, value_rows.astype(jnp.float32), precision=lax.Precision.HIGHEST)
    return (blended / jnp.transpose(sums_row)[:, :, None]).astype(jnp.bfloat16)

def reference(latent, text_tokens, mod_shift, mod_scale, mod_gate, project_in, project_out, q_gain, k_gain, pattern, tile_rows, text_mask):
    time_tiles = F // TF
    row_tiles = H // TH
    band_count = W // TW
    per_device = time_tiles * row_tiles
    tile_size = TF * TH * TW
    tile_total = per_device * band_count
    flat_in = project_in.reshape(D, 3 * HEADS * HD)

    def prepare(token_rows):
        product = jnp.dot(modulate(token_rows, mod_shift, mod_scale), flat_in, preferred_element_type=jnp.float32)
        product = product.reshape(token_rows.shape[0], 3, HEADS, HD)
        return (rms_gain(product[:, 0], q_gain), rms_gain(product[:, 1], k_gain), product[:, 2].astype(jnp.bfloat16))
    arranged = latent.reshape(time_tiles, TF, row_tiles, TH, band_count, TW, D)
    arranged = jnp.transpose(arranged, (4, 0, 2, 1, 3, 5, 6)).reshape(tile_total, tile_size, D)
    tile_queries, tile_keys, tile_values = lax.map(prepare, arranged)
    text_queries, text_keys, text_values = prepare(text_tokens)
    positions = jnp.arange(tile_size, dtype=jnp.int32)
    tile_usable = positions[None, :] < tile_rows[:, None]
    text_usable = text_mask == 1
    owners = jnp.arange(tile_total, dtype=jnp.int32) // per_device
    key_tiles = ((owners[:, None] + pattern // per_device - 1) * per_device + pattern % per_device).astype(jnp.int32)

    def latent_tile(tile_id):
        chosen = key_tiles[tile_id]
        key_rows = jnp.concatenate([tile_keys[chosen].reshape(-1, HEADS, HD), text_keys], 0)
        value_rows = jnp.concatenate([tile_values[chosen].reshape(-1, HEADS, HD), text_values], 0)
        usable = jnp.concatenate([tile_usable[chosen].reshape(-1), text_usable], 0)
        return attend(tile_queries[tile_id], key_rows, value_rows, usable)
    latent_out = lax.map(latent_tile, jnp.arange(tile_total, dtype=jnp.int32))
    latent_out = jnp.where(tile_usable[:, :, None, None], latent_out, jnp.zeros_like(latent_out))
    every_keys = jnp.concatenate([tile_keys.reshape(-1, HEADS, HD), text_keys], 0)
    every_values = jnp.concatenate([tile_values.reshape(-1, HEADS, HD), text_values], 0)
    every_usable = jnp.concatenate([tile_usable.reshape(-1), text_usable], 0)

    def text_head(head_id):

        def select_head(source):
            return lax.dynamic_slice_in_dim(source, head_id, 1, 1)
        return attend(select_head(text_queries), select_head(every_keys), select_head(every_values), every_usable)[:, 0]
    text_out = jnp.transpose(lax.map(text_head, jnp.arange(HEADS, dtype=jnp.int32)), (1, 0, 2))
    group_width = HEADS * HD // N_HEAD

    def out_project(attention_rows):
        accum = jnp.zeros((attention_rows.shape[0], D), jnp.float32)
        for group_id in range(N_HEAD):
            lower = group_id * group_width
            partial_term = jnp.dot(attention_rows[:, lower:lower + group_width], project_out[lower:lower + group_width], preferred_element_type=jnp.float32)
            accum = accum + lax.optimization_barrier(partial_term.astype(jnp.bfloat16)).astype(jnp.float32)
        return (accum * mod_gate).astype(jnp.bfloat16)
    latent_rows = out_project(latent_out.reshape(-1, HEADS * HD))
    update = latent_rows.reshape(band_count, time_tiles, row_tiles, TF, TH, TW, D)
    update = jnp.transpose(update, (1, 3, 2, 4, 0, 5, 6)).reshape(F, H, W, D)
    text_update = out_project(text_out.reshape(TEXT, HEADS * HD))
    return (update, text_update)
```

```python
import functools
import math

import jax
import jax.numpy as jnp
from jax import lax
from jax.experimental import pallas as pl
from jax.experimental.pallas import tpu as pltpu
from jax.sharding import PartitionSpec as P

D = 3072
HD = 128
F = 16
H = 6
TW = 8
TEXT = 256
GROUPS = 4
EPSILON = 1e-06
NEG = -1e30
FACTOR = math.log2(math.e) / math.sqrt(HD)
LN2 = math.log(2.0)
F32 = jnp.float32
BF16 = jnp.bfloat16


def spec(shape, index_map, single=False):
    if single:
        return pl.BlockSpec(shape, index_map, pipeline_mode=pl.Buffered(1))
    return pl.BlockSpec(shape, index_map)


def xor(count, k):
    return [(i, i ^ k) for i in range(count)]


def shift(count, s):
    return [(i, (i + s) % count) for i in range(count)]


def rms(values, gain):
    square = jnp.mean(values * values, axis=-1, keepdims=True)
    return (values * lax.rsqrt(square + EPSILON) * gain).astype(BF16)


def project_kernel(parts, rows, count, ordered, pos, *refs):
    shards = refs[:count]
    shift_ref, scale_ref, w_ref, q_gain, k_gain, normed_ref, out_ref = refs[count:]
    which = lax.rem(pl.program_id(0) + 1, 3)
    width = shards[0].shape[1]
    step = 16

    @pl.when((pl.program_id(0) == 0) & (pl.program_id(1) == 0))
    def _():
        def block(i, carry):
            start = pl.multiple_of(i * step, step)
            if parts == 1:
                target = start
            else:
                part = start // rows
                source = lax.rem(pos[0] - part + parts, parts)
                target = pl.multiple_of(source * rows + start - part * rows, step)
            wide = [ref[pl.ds(start, step), :].astype(F32) for ref in shards]
            total = jnp.sum(sum(wide), axis=-1, keepdims=True)
            center = total / D
            offset = [x - center for x in wide]
            variance = jnp.sum(sum(x * x for x in offset), axis=-1, keepdims=True) / D
            inverse = lax.rsqrt(variance + EPSILON)
            for k in range(count):
                owner = k if ordered else pos[1] ^ k
                column = pl.ds(pl.multiple_of(owner * width, 128), width)
                normed_ref[pl.ds(target, step), column] = (
                    offset[k] * inverse * (1.0 + scale_ref[:, column]) + shift_ref[:, column]
                ).astype(BF16)
            return carry

        lax.fori_loop(0, parts * rows // step, block, 0, unroll=4)

    product = jnp.dot(normed_ref[...], w_ref[0], preferred_element_type=F32)
    gain = jnp.where(which == 0, q_gain[...], k_gain[...])
    for i in range(out_ref.shape[1]):
        piece = product[:, i * HD : (i + 1) * HD]

        @pl.when(which == 2)
        def _():
            out_ref[0, i] = piece.astype(BF16)

        @pl.when(which != 2)
        def _():
            out_ref[0, i] = rms(piece, gain)


def project(shards, shard_specs, pos, parts, rows, kinds, ordered, mod_shift, mod_scale, weights, q_gain, k_gain):
    count = len(shards)
    tokens = parts * rows
    width = weights.shape[2]
    block = 384 if width % 384 == 0 else HD
    heads = width // HD
    whole = lambda c, j, s: (0, 0)
    return pl.pallas_call(
        functools.partial(project_kernel, parts, rows, count, ordered),
        out_shape=(
            jax.ShapeDtypeStruct((tokens, D), BF16),
            jax.ShapeDtypeStruct((kinds, heads, tokens, HD), BF16),
        ),
        grid_spec=pltpu.PrefetchScalarGridSpec(
            num_scalar_prefetch=1,
            grid=(kinds, width // block),
            in_specs=shard_specs
            + [
                spec((1, D), whole, True),
                spec((1, D), whole, True),
                spec((1, D, block), lambda c, j, s: (lax.rem(c + 1, 3), 0, j)),
                spec((1, HD), whole, True),
                spec((1, HD), whole, True),
            ],
            out_specs=(
                spec((tokens, D), whole),
                spec((1, block // HD, tokens, HD), lambda c, j, s: (c, j, 0, 0)),
            ),
        ),
        cost_estimate=pl.CostEstimate(
            flops=2 * tokens * D * width * kinds,
            bytes_accessed=2 * (2 * tokens * D + kinds * width * (D + tokens)),
            transcendentals=0,
        ),
        name="project",
    )(pos, *shards, mod_shift, mod_scale, weights, q_gain, k_gain)


def query_kernel(count, *refs):
    normed = refs[:count]
    w_ref, q_gain = refs[count : count + 2]
    outs = refs[count + 2 :]
    for c in range(count):
        product = jnp.dot(normed[c][...], w_ref[0], preferred_element_type=F32)
        for i in range(outs[c].shape[0]):
            outs[c][i] = rms(product[:, i * HD : (i + 1) * HD], q_gain[...])


def queries(normed, weights, q_gain):
    count = len(normed)
    tokens = normed[0].shape[0]
    width = weights.shape[2]
    block = 384 if width % 384 == 0 else HD
    return pl.pallas_call(
        functools.partial(query_kernel, count),
        out_shape=[jax.ShapeDtypeStruct((width // HD, tokens, HD), BF16)] * count,
        grid=(width // block,),
        in_specs=[spec((tokens, D), lambda j: (0, 0), True)] * count
        + [
            spec((1, D, block), lambda j: (0, 0, j)),
            spec((1, HD), lambda j: (0, 0), True),
        ],
        out_specs=[spec((block // HD, tokens, HD), lambda j: (j, 0, 0))] * count,
        cost_estimate=pl.CostEstimate(
            flops=2 * tokens * count * D * width,
            bytes_accessed=2 * (count * tokens * (D + width) + width * D),
            transcendentals=0,
        ),
        name="queries",
    )(*normed, weights, q_gain)


def scores_of(query, key, bias):
    return (
        lax.dot_general(query, key, (((1,), (1,)), ((), ())), preferred_element_type=F32) + bias
    )


def with_ones(value):
    return jnp.concatenate([value, jnp.ones_like(value)], 1)


def softmax_parts(jobs):
    scores = scores_of(jobs[0][0], jobs[0][1], jobs[0][3])
    for number, (_, _, value, _) in enumerate(jobs):
        ahead = None
        if number + 1 < len(jobs):
            ahead = scores_of(jobs[number + 1][0], jobs[number + 1][1], jobs[number + 1][3])
        highest = jnp.max(scores, axis=-1, keepdims=True)
        weights = jnp.exp2((scores - highest) * FACTOR).astype(BF16)
        both = jnp.dot(weights, value, preferred_element_type=F32)
        yield highest * FACTOR, both[:, :HD], both[:, HD:]
        scores = ahead


def tile_bias(count, chunks, half, rows, span):
    place = lax.broadcasted_iota(jnp.int32, (1, half), 1)
    place = place // rows * span + lax.rem(place, rows)
    return jnp.concatenate(
        [jnp.where(place + c * rows < count, 0.0, NEG) for c in range(chunks)], 1
    )


def text_bias(mask_ref):
    return jnp.where(mask_ref[...] == 1, 0.0, NEG)


def heads_at_once(heads):
    return 2 if heads % 2 == 0 else 1


def own_kernel(chunks, parts, pos, tile_rows, *refs):
    q_refs = refs[:chunks]
    kv_refs = refs[chunks : 2 * chunks]
    text_ref, mask_ref, out_ref, log_ref = refs[2 * chunks :]
    half = q_refs[0].shape[1] // 2
    rows = 2 * half // parts
    span = F // parts * H * TW
    jobs, places = [], []
    text = text_bias(mask_ref)
    size = half // 2 if half % 32 == 0 else half
    for a in range(2):
        bias = jnp.concatenate(
            [tile_bias(tile_rows[pos[0] * 2 + a], chunks, half, rows, span), text], 1
        )
        own = slice(a * half, (a + 1) * half)
        for h in range(q_refs[0].shape[0]):
            key = jnp.concatenate([ref[0, h, own, :] for ref in kv_refs] + [text_ref[0, h]], 0)
            value = with_ones(
                jnp.concatenate([ref[1, h, own, :] for ref in kv_refs] + [text_ref[1, h]], 0)
            )
            for c in range(chunks):
                for low in range(a * half, (a + 1) * half, size):
                    mine = slice(low, low + size)
                    jobs.append((q_refs[c][h, mine, :], key, value, bias))
                    places.append((h, c, mine))
    for (h, c, mine), (highest, blended, total) in zip(places, softmax_parts(jobs)):
        out_ref[h, c, mine, :] = blended / total
        log_ref[h, c, mine, :] = highest + jnp.log(total) / LN2


def own_attention(pos, tile_rows, q_list, kv_list, text_kv, mask, parts):
    chunks = len(q_list)
    heads, tokens, _ = q_list[0].shape
    state = jax.ShapeDtypeStruct((heads, chunks, tokens, HD), F32)
    keys = chunks * tokens // 2 + TEXT
    hb = heads_at_once(heads)
    return pl.pallas_call(
        functools.partial(own_kernel, chunks, parts),
        out_shape=(state, state),
        grid_spec=pltpu.PrefetchScalarGridSpec(
            num_scalar_prefetch=2,
            grid=(heads // hb,),
            in_specs=[spec((hb, tokens, HD), lambda h, *_: (h, 0, 0))] * chunks
            + [spec((2, hb, tokens, HD), lambda h, *_: (0, h, 0, 0))] * chunks
            + [
                spec((2, hb, TEXT, HD), lambda h, *_: (0, h, 0, 0)),
                spec((1, TEXT), lambda h, *_: (0, 0), True),
            ],
            out_specs=(spec((hb, chunks, tokens, HD), lambda h, *_: (h, 0, 0, 0)),) * 2,
        ),
        cost_estimate=pl.CostEstimate(
            flops=4 * heads * chunks * tokens * keys * HD,
            bytes_accessed=heads * chunks * tokens * HD * 16,
            transcendentals=heads * chunks * tokens * keys,
        ),
        name="own_attention",
    )(pos, tile_rows, *q_list, *kv_list, text_kv, mask)


def tile_kernel(chunks, targets, blocks, parts, pos, tile_rows, pattern, *refs):
    q_refs = refs[:chunks]
    sides = refs[chunks : 4 * chunks]
    out_state, log_state = refs[4 * chunks : 4 * chunks + 2]
    outs = refs[4 * chunks + 2 : -2]
    buffer, sems = refs[-2:]
    at_once, tokens, _ = q_refs[0].shape
    half = tokens // 2
    rows = tokens // parts
    span = F // parts * H * TW
    band, this = pos[0], pos[1]
    tile = (this ^ targets[0]) * blocks // (parts // 2)
    slots = [pattern[tile, e + 1] for e in range(3)]
    first_head = pl.program_id(0) * at_once

    def copies(h, wait):
        for e in range(3):
            start = pl.multiple_of(lax.rem(slots[e], 2) * half, half)
            for side in range(3):

                @pl.when(slots[e] // 2 == side)
                def _():
                    for c in range(chunks):
                        copy = pltpu.make_async_copy(
                            sides[side * chunks + c].at[:, h, pl.ds(start, half), :],
                            buffer.at[h, :, pl.ds((e * chunks + c) * half, half), :],
                            sems.at[h, e, c],
                        )
                        if wait:
                            copy.wait()
                        else:
                            copy.start()

    @pl.when(pl.program_id(0) == 0)
    def _():
        for h in range(buffer.shape[0]):
            copies(h, False)

    for h in range(at_once):
        copies(first_head + h, True)
    bias = jnp.concatenate(
        [
            tile_bias(
                tile_rows[(band + slot // 2 - 1) * 2 + lax.rem(slot, 2)], chunks, half, rows, span
            )
            for slot in slots
        ],
        1,
    )
    jobs, places = [], []
    for h in range(at_once):
        key = buffer[first_head + h, 0]
        value = with_ones(buffer[first_head + h, 1])
        for t, k in enumerate(targets):
            for c in range(chunks):
                for i in range(blocks):
                    source = (this ^ k) * blocks + i
                    at = pl.ds(pl.multiple_of(source * rows, 16), rows)
                    jobs.append((q_refs[c][h, at, :], key, value, bias))
                    places.append((h, t, c, i, source, at))
    real = tile_rows[band * 2 + tile]
    for (h, t, c, i, source, at), (top, blended, total) in zip(places, softmax_parts(jobs)):
        log = log_state[h, c, at, :]
        most = jnp.maximum(log, top)
        first = jnp.exp2(log - most)
        second = jnp.exp2(top - most)
        result = (out_state[h, c, at, :] * first + blended * second) / (first + total * second)
        place = (
            lax.rem(source, parts // 2) * span
            + c * rows
            + lax.broadcasted_iota(jnp.int32, result.shape, 0)
        )
        low = (c * blocks + i) * rows
        outs[t][low : low + rows, h * HD : (h + 1) * HD] = jnp.where(
            place < real, result, 0.0
        ).astype(BF16)


def tile_attention(pos, tile_rows, pattern, q_list, sides, states, targets, blocks, parts):
    chunks = len(q_list)
    heads, tokens, _ = q_list[0].shape
    rows = tokens // parts * blocks * chunks
    keys = 3 * chunks * tokens // 2
    hb = heads_at_once(heads)
    return pl.pallas_call(
        functools.partial(tile_kernel, chunks, targets, blocks, parts),
        out_shape=[jax.ShapeDtypeStruct((rows, heads * HD), BF16)] * len(targets),
        grid_spec=pltpu.PrefetchScalarGridSpec(
            num_scalar_prefetch=3,
            grid=(heads // hb,),
            in_specs=[spec((hb, tokens, HD), lambda h, *_: (h, 0, 0))] * chunks
            + [pl.BlockSpec(memory_space=pl.ANY)] * (3 * chunks)
            + [spec((hb, chunks, tokens, HD), lambda h, *_: (h, 0, 0, 0))] * 2,
            out_specs=[spec((rows, hb * HD), lambda h, *_: (0, h))] * len(targets),
            scratch_shapes=[
                pltpu.VMEM((heads, 2, keys, HD), BF16),
                pltpu.SemaphoreType.DMA((heads, 3, chunks)),
            ],
        ),
        cost_estimate=pl.CostEstimate(
            flops=4 * heads * rows * len(targets) * keys * HD,
            bytes_accessed=heads * (keys * HD * 4 + chunks * tokens * HD * 10),
            transcendentals=heads * rows * len(targets) * keys,
        ),
        name="tile_attention",
    )(pos, tile_rows, pattern, *q_list, *sides, *states)


def text_kernel(chunks, parts, pos, tile_rows, *refs):
    kv_refs = refs[:chunks]
    q_ref, text_ref, mask_ref, out_ref = refs[chunks:]
    at_once, tokens, _ = kv_refs[0].shape[1:]
    half = tokens // 2
    rows = tokens // parts
    span = F // parts * H * TW
    first_head = pl.program_id(0) * at_once
    width = out_ref.shape[1] - HD
    own = [tile_bias(tile_rows[pos[0] * 2 + a], chunks, half, rows, span) for a in range(2)]
    bias = jnp.concatenate(
        [own[a][:, c * half : (c + 1) * half] for c in range(chunks) for a in range(2)]
        + [jnp.where(pos[0] == 0, text_bias(mask_ref), NEG)],
        1,
    )
    size = 64
    jobs, places = [], []
    for h in range(at_once):
        key = jnp.concatenate([ref[0, h] for ref in kv_refs] + [text_ref[0, h]], 0)
        value = with_ones(jnp.concatenate([ref[1, h] for ref in kv_refs] + [text_ref[1, h]], 0))
        for low in range(0, TEXT, size):
            jobs.append((q_ref[0, h, low : low + size, :], key, value, bias))
            places.append((h, slice(low, low + size)))

    @pl.when(pl.program_id(0) == 0)
    def _():
        out_ref[:, width:] = jnp.zeros((TEXT, HD), BF16)

    for (h, mine), (highest, blended, total) in zip(places, softmax_parts(jobs)):
        head = first_head + h
        out_ref[mine, pl.ds(pl.multiple_of(head * HD, HD), HD)] = (blended / total).astype(BF16)
        log = highest + jnp.log(total) / LN2
        lane = lax.broadcasted_iota(jnp.int32, log.shape, 1)
        stats = out_ref[mine, width:].astype(F32)
        for i in range(3):
            term = log.astype(BF16).astype(F32)
            stats = jnp.where(lane == 3 * head + i, term, stats)
            log = log - term
        out_ref[mine, width:] = stats.astype(BF16)


def text_attention(pos, tile_rows, kv_list, text_qkv, mask, parts):
    chunks = len(kv_list)
    _, heads, tokens, _ = kv_list[0].shape
    width = heads * HD
    keys = chunks * tokens + TEXT
    hb = heads_at_once(heads)
    return pl.pallas_call(
        functools.partial(text_kernel, chunks, parts),
        out_shape=jax.ShapeDtypeStruct((TEXT, width + HD), BF16),
        grid_spec=pltpu.PrefetchScalarGridSpec(
            num_scalar_prefetch=2,
            grid=(heads // hb,),
            in_specs=[spec((2, hb, tokens, HD), lambda h, *_: (0, h, 0, 0))] * chunks
            + [
                spec((1, hb, TEXT, HD), lambda h, *_: (2, h, 0, 0)),
                spec((2, hb, TEXT, HD), lambda h, *_: (0, h, 0, 0)),
                spec((1, TEXT), lambda h, *_: (0, 0), True),
            ],
            out_specs=spec((TEXT, width + HD), lambda h, *_: (0, 0)),
        ),
        cost_estimate=pl.CostEstimate(
            flops=4 * heads * TEXT * keys * HD,
            bytes_accessed=4 * width * (chunks * tokens + TEXT),
            transcendentals=heads * TEXT * keys,
        ),
        name="text_attention",
    )(pos, tile_rows, *kv_list, text_qkv, text_qkv, mask)


def merge_kernel(*refs):
    parts, out_ref = refs[:-1], refs[-1]
    width = out_ref.shape[1]
    for h in range(width // HD):
        logs = [
            sum(ref[:, width + 3 * h + i : width + 3 * h + i + 1].astype(F32) for i in range(3))
            for ref in parts
        ]
        most = functools.reduce(jnp.maximum, logs)
        factors = [jnp.exp2(log - most) for log in logs]
        column = slice(h * HD, (h + 1) * HD)
        total = sum(factors)
        blended = sum(f * ref[:, column].astype(F32) for f, ref in zip(factors, parts))
        out_ref[:, column] = (blended / total).astype(BF16)


def merge_text(parts):
    rows, wide = parts[0].shape
    return pl.pallas_call(
        merge_kernel,
        out_shape=jax.ShapeDtypeStruct((rows, wide - HD), BF16),
        name="merge_text",
    )(*parts)


def output_kernel(count, layout, pos, *refs):
    latent_refs = refs[:count]
    text_refs = refs[count : 2 * count]
    pieces = refs[2 * count : 2 * count + len(layout)]
    gate_ref, update_ref, text_update_ref, held = refs[2 * count + len(layout) :]
    rows = update_ref.shape[0]

    @pl.when(pl.program_id(0) == 0)
    def _():
        for k in range(count):
            held[k, :rows] = latent_refs[k][...]
            held[k, rows:] = text_refs[k][...]

    terms = {}
    for (k, low, moves, group), w_ref in zip(layout, pieces):
        column = pl.ds(low, w_ref.shape[0])
        if moves:
            column = pl.ds(pl.multiple_of(low + pos[2] * moves, 128), w_ref.shape[0])
        term = jnp.dot(held[k, :, column], w_ref[...], preferred_element_type=F32)
        terms[group] = terms[group] + term if group in terms else term
    total = sum(term.astype(BF16).astype(F32) for term in terms.values())
    result = (total * gate_ref[...]).astype(BF16)
    update_ref[...] = result[:rows]
    text_update_ref[...] = result[rows:]


def output(pos, latent_parts, text_parts, weights, groups, gate):
    count = len(latent_parts)
    rows, width = latent_parts[0].shape
    text_rows = text_parts[0].shape[0]
    block = 512
    layout = [(k, low, moves, groups[k]) for k, low, moves, _ in weights]
    return pl.pallas_call(
        functools.partial(output_kernel, count, layout),
        out_shape=(
            jax.ShapeDtypeStruct((rows, D), BF16),
            jax.ShapeDtypeStruct((text_rows, D), BF16),
        ),
        grid_spec=pltpu.PrefetchScalarGridSpec(
            num_scalar_prefetch=1,
            grid=(D // block,),
            in_specs=[spec((rows, width), lambda j, *_: (0, 0), True)] * count
            + [spec((text_rows, width), lambda j, *_: (0, 0), True)] * count
            + [spec((w.shape[0], block), lambda j, *_: (0, j)) for _, _, _, w in weights]
            + [spec((1, block), lambda j, *_: (0, j))],
            out_specs=(
                spec((rows, block), lambda j, *_: (0, j)),
                spec((text_rows, block), lambda j, *_: (0, j)),
            ),
            scratch_shapes=[pltpu.VMEM((count, rows + text_rows, width), BF16)],
        ),
        cost_estimate=pl.CostEstimate(
            flops=2 * (rows + text_rows) * D * D,
            bytes_accessed=2 * D * (D + 2 * (rows + text_rows)),
            transcendentals=0,
        ),
        name="output",
    )(pos, *latent_parts, *text_parts, *[w for _, _, _, w in weights], gate)


def after(value, *others):
    return lax.optimization_barrier((value,) + others)[0]


def shards(
    latent,
    text_tokens,
    mod_shift,
    mod_scale,
    mod_gate,
    project_in,
    project_out,
    q_gain,
    k_gain,
    pattern,
    tile_rows,
    text_mask,
):
    heads = lax.axis_size("head")
    bands = lax.axis_size("tile")
    this = lax.axis_index("head")
    band = lax.axis_index("tile")
    width = latent.shape[3]
    frames = latent.shape[0]
    chunks = 2 if frames % 2 == 0 else 1
    step = frames // chunks
    rows = step * H * TW
    tokens = bands * rows
    blocks = F // heads // frames
    assert blocks >= 1 and (blocks == 1 or chunks == 1) and heads & (heads - 1) == 0

    weights = jnp.transpose(project_in, (1, 0, 2))
    mod_shift = mod_shift[None, :]
    mod_scale = mod_scale[None, :]
    q_gain = q_gain[None, :]
    k_gain = k_gain[None, :]
    mask = text_mask[None, :]
    pos = jnp.stack([band, this, lax.axis_index("group")]).astype(jnp.int32)
    norm = (mod_shift, mod_scale, weights, q_gain, k_gain)
    groups = lax.axis_size("group")

    split = groups == 2 and width % 768 == 0
    half_width = width // 2
    pieces = ((0, width // 3), (width // 3, half_width - width // 3)) if split else ((0, width),)
    group = lax.axis_index("group") if split else 0
    own_weights = [
        lax.dynamic_slice_in_dim(project_out, group * half_width + low, size, 0)
        if split
        else project_out
        for low, size in pieces
    ]
    crossed = {}
    for k in range(2, heads, 2):
        for p, piece in enumerate(own_weights):
            crossed[k, p, 0] = lax.ppermute(piece, "head", xor(heads, k))
            if split:
                crossed[k, p, 1] = lax.ppermute(crossed[k, p, 0], "group", xor(2, 1))

    _, text_qkv = project(
        [text_tokens] * heads,
        [
            spec((TEXT, width), functools.partial(lambda k, c, j, s: (0, k), k), True)
            for k in range(heads)
        ],
        pos,
        1,
        TEXT,
        3,
        True,
        *norm,
    )

    parts = []
    for c in range(chunks):
        own = latent[c * step : (c + 1) * step]

        def piece(s):
            at = lax.rem(band + s, bands) * TW
            return lax.dynamic_slice_in_dim(own, at, TW, 2).reshape(rows, width)

        parts.append(
            [piece(0)]
            + [lax.ppermute(piece(s), "tile", shift(bands, s)) for s in range(1, bands)]
        )
    gathered = []
    for c in range(chunks):
        mine = jnp.concatenate(after(parts[c], text_qkv), 0)
        received = {0: mine}
        for k in range(2, heads, 2):
            received[k] = lax.ppermute(mine, "head", xor(heads, k))
        for k in range(0, heads, 2):
            received[k + 1] = lax.ppermute(received[k], "head", xor(heads, 1))
        gathered.append([received[k] for k in range(heads)])

    normed, kv = [], []
    for c in range(chunks):
        normed_part, kv_part = project(
            gathered[c],
            [spec((tokens, width), lambda c, j, s: (0, 0), True)] * heads,
            pos,
            bands,
            rows,
            2,
            False,
            *norm,
        )
        normed.append(normed_part)
        kv.append(kv_part)

    forward = [(i, i + 1) for i in range(bands - 1)]
    backward = [(i + 1, i) for i in range(bands - 1)]
    low = [lax.ppermute(part, "tile", forward) for part in kv]
    high = [lax.ppermute(part, "tile", backward) for part in kv]

    share = text_attention(pos, tile_rows, kv, text_qkv, mask, bands)
    count = TEXT // bands

    def text_piece(s):
        return lax.dynamic_slice_in_dim(share, lax.rem(band + s, bands) * count, count, 0)

    text_part = merge_text(
        [text_piece(0)]
        + [lax.ppermute(text_piece(s), "tile", shift(bands, s)) for s in range(1, bands)],
    )
    everyone = [text_part] + [
        lax.ppermute(text_part, "tile", shift(bands, s)) for s in range(1, bands)
    ]
    ordered = jnp.concatenate(everyone[::-1] + everyone[:0:-1], 0)
    text_out = lax.dynamic_slice_in_dim(ordered, (bands - 1 - band) * count, TEXT, 0)
    text_rows = TEXT // heads
    text_parts = []
    for k in range(heads):
        part = lax.dynamic_slice_in_dim(text_out, (this ^ k) * text_rows, text_rows, 0)
        text_parts.append(lax.ppermute(part, "head", xor(heads, k)) if k else part)

    q_list = queries(normed, weights, q_gain)
    states = own_attention(pos, tile_rows, q_list, kv, text_qkv, mask, bands)

    latent_parts = {}
    for far in (1, 0):
        targets = [k for k in range(heads) if k // (heads // 2) == far]
        outs = tile_attention(
            pos, tile_rows, pattern, q_list, low + kv + high, states, targets, blocks, bands
        )
        for k, part in zip(targets, outs):
            latent_parts[k] = lax.ppermute(part, "head", xor(heads, k)) if k else part

    held = [(0, 0, 0, project_out), (1, 0, 0, lax.ppermute(project_out, "head", xor(heads, 1)))]
    for (k, p, far), value in crossed.items():
        partner = lax.ppermute(value, "head", xor(heads, 1))
        start = pieces[p][0]
        moves = (1 if far == 0 else -1) * half_width if split else 0
        base = half_width if split and far else 0
        held += [(k, base + start, moves, value), (k + 1, base + start, moves, partner)]

    update, text_update = output(
        pos,
        [latent_parts[k] for k in range(heads)],
        text_parts,
        held,
        [k * GROUPS // heads for k in range(heads)],
        mod_gate[None, :],
    )
    return (update.reshape(F // heads, H, TW, D), text_update)


def solution(mesh):
    placed = (
        P(("group", "tile"), None, None, "head"),
        P("group", None),
        P(),
        P(),
        P(),
        P(None, None, "head"),
        P("head", None),
        P(),
        P(),
        P("tile", None),
        P("group"),
        P("group"),
    )
    return jax.shard_map(
        shards,
        mesh=mesh,
        in_specs=placed,
        out_specs=(P(("group", "head"), None, "tile", None), P(("group", "head"), None)),
        check_vma=False,
    )
```

```python
import functools
import math

import jax
import jax.numpy as jnp
from jax import lax
from jax.experimental import pallas as pl
from jax.experimental.pallas import tpu as pltpu
from jax.sharding import PartitionSpec as P

D = 3072
HD = 128
F = 16
H = 6
TW = 8
TEXT = 256
GROUPS = 4
EPSILON = 1e-06
NEG = -1e30
VMEM = 58 << 20
JOB = 384
FACTOR = math.log2(math.e) / math.sqrt(HD)
LN2 = math.log(2.0)
F32 = jnp.float32
BF16 = jnp.bfloat16


def spec(shape, index_map, single=False):
    if single:
        return pl.BlockSpec(shape, index_map, pipeline_mode=pl.Buffered(1))
    return pl.BlockSpec(shape, index_map)


def xor(count, k):
    return [(i, i ^ k) for i in range(count)]


def shift(count, s):
    return [(i, (i + s) % count) for i in range(count)]


def rms(values, gain):
    square = jnp.mean(values * values, axis=-1, keepdims=True)
    return (values * lax.rsqrt(square + EPSILON) * gain).astype(BF16)


def project_kernel(parts, rows, count, ordered, pos, *refs):
    shards = refs[:count]
    shift_ref, scale_ref, weights, q_gain, k_gain, kv_ref, q_ref, normed, held, sems = refs[count:]
    width = shards[0].shape[1]
    step = 16
    block = 256 if width % 256 == 0 else HD
    loads = sems.shape[1]
    deep = D // loads

    def load(c, j):
        low = pl.ds(j * deep, deep)
        return pltpu.make_async_copy(
            weights.at[(c + 1) % 3, low], held.at[c, low], sems.at[c, j]
        )

    for c in range(3):
        for j in range(loads):
            load(c, j).start()

    def norm(i, carry):
        start = pl.multiple_of(i * step, step)
        if parts == 1:
            target = start
        else:
            part = start // rows
            source = lax.rem(pos[0] - part + parts, parts)
            target = pl.multiple_of(source * rows + start - part * rows, step)
        wide = [ref[pl.ds(start, step), :].astype(F32) for ref in shards]
        total = jnp.sum(sum(wide), axis=-1, keepdims=True)
        center = total / D
        offset = [x - center for x in wide]
        variance = jnp.sum(sum(x * x for x in offset), axis=-1, keepdims=True) / D
        inverse = lax.rsqrt(variance + EPSILON)
        for k in range(count):
            owner = k if ordered else pos[1] ^ k
            column = pl.ds(pl.multiple_of(owner * width, 128), width)
            normed[pl.ds(target, step), column] = (
                offset[k] * inverse * (1.0 + scale_ref[:, column]) + shift_ref[:, column]
            ).astype(BF16)
        return carry

    lax.fori_loop(0, parts * rows // step, norm, 0, unroll=4)

    per_block = block // HD
    for c in range(3):
        for j in range(loads):
            load(c, j).wait()
        for j in range(width // block):
            product = jnp.dot(
                normed[...], held[c, :, j * block : (j + 1) * block], preferred_element_type=F32
            )
            for i in range(per_block):
                head = j * per_block + i
                piece = product[:, i * HD : (i + 1) * HD]
                if c == 0:
                    kv_ref[0, head] = rms(piece, k_gain[...])
                elif c == 1:
                    kv_ref[1, head] = piece.astype(BF16)
                else:
                    q_ref[head] = rms(piece, q_gain[...])


def project(shards, shard_specs, pos, parts, rows, ordered, mod_shift, mod_scale, weights, q_gain, k_gain):
    count = len(shards)
    tokens = parts * rows
    width = weights.shape[2]
    heads = width // HD
    whole = lambda c, s: (0, 0)
    return pl.pallas_call(
        functools.partial(project_kernel, parts, rows, count, ordered),
        out_shape=(
            jax.ShapeDtypeStruct((2, heads, tokens, HD), BF16),
            jax.ShapeDtypeStruct((heads, tokens, HD), BF16),
        ),
        grid_spec=pltpu.PrefetchScalarGridSpec(
            num_scalar_prefetch=1,
            grid=(1,),
            in_specs=shard_specs
            + [
                spec((1, D), whole, True),
                spec((1, D), whole, True),
                pl.BlockSpec(memory_space=pl.ANY),
                spec((1, HD), whole, True),
                spec((1, HD), whole, True),
            ],
            out_specs=(
                spec((2, heads, tokens, HD), lambda c, s: (0, 0, 0, 0)),
                spec((heads, tokens, HD), lambda c, s: (0, 0, 0)),
            ),
            scratch_shapes=[
                pltpu.VMEM((tokens, D), BF16),
                pltpu.VMEM((3, D, width), BF16),
                pltpu.SemaphoreType.DMA((3, 4)),
            ],
        ),
        compiler_params=pltpu.CompilerParams(vmem_limit_bytes=VMEM),
        cost_estimate=pl.CostEstimate(
            flops=6 * tokens * D * width,
            bytes_accessed=2 * (2 * tokens * D + 3 * width * (D + tokens)),
            transcendentals=0,
        ),
        name="project",
    )(pos, *shards, mod_shift, mod_scale, weights, q_gain, k_gain)


def scores_of(query, key, bias):
    return (
        lax.dot_general(query, key, (((1,), (1,)), ((), ())), preferred_element_type=F32) + bias
    )


def with_ones(value):
    return jnp.concatenate([value, jnp.ones_like(value)], 1)


def softmax_parts(jobs):
    scores = scores_of(jobs[0][0], jobs[0][1], jobs[0][3])
    for number, (_, _, value, _) in enumerate(jobs):
        ahead = None
        if number + 1 < len(jobs):
            ahead = scores_of(jobs[number + 1][0], jobs[number + 1][1], jobs[number + 1][3])
        highest = jnp.max(scores, axis=-1, keepdims=True)
        weights = jnp.exp2((scores - highest) * FACTOR).astype(BF16)
        both = jnp.dot(weights, value, preferred_element_type=F32)
        yield highest * FACTOR, both[:, :HD], both[:, HD:]
        scores = ahead


def tile_bias(count, chunks, half, rows, span):
    place = lax.broadcasted_iota(jnp.int32, (1, half), 1)
    place = place // rows * span + lax.rem(place, rows)
    return jnp.concatenate(
        [jnp.where(place + c * rows < count, 0.0, NEG) for c in chunks], 1
    )


def text_bias(mask_ref):
    return jnp.where(mask_ref[...] == 1, 0.0, NEG)


def gather(sides, slots, half, buffer, sems, wait):
    count = len(sides) // 3
    for e, slot in enumerate(slots):
        start = pl.multiple_of(lax.rem(slot, 2) * half, half)
        for side in range(3):

            @pl.when(slot // 2 == side)
            def _():
                for c in range(count):
                    copy = pltpu.make_async_copy(
                        sides[side * count + c].at[:, pl.ds(start, half), :],
                        buffer.at[:, pl.ds((e * count + c) * half, half), :],
                        sems.at[e, c],
                    )
                    if wait:
                        copy.wait()
                    else:
                        copy.start()


def others_bias(tile_rows, band, slots, chunks, half, rows, span):
    return [
        tile_bias(
            tile_rows[(band + slot // 2 - 1) * 2 + lax.rem(slot, 2)], chunks, half, rows, span
        )
        for slot in slots
    ]


def heads_at_once(heads):
    return 2 if heads % 2 == 0 else 1


def own_kernel(chunks, parts, early, pos, tile_rows, pattern, *refs):
    q_refs = refs[:chunks]
    kv_refs = refs[chunks : 2 * chunks]
    sides = refs[2 * chunks : 2 * chunks + 3 * early]
    text_ref, mask_ref, out_ref, log_ref = refs[2 * chunks + 3 * early :][:4]
    at_once, tokens, _ = q_refs[0].shape
    half = tokens // 2
    rows = tokens // parts
    span = F // parts * H * TW
    first_head = pl.program_id(0) * at_once
    slots = [[pattern[a, e + 1] for e in range(3)] for a in range(2)]
    if early:
        buffer, sems = refs[-2:]

        def copies(h, wait):
            for a in range(2):
                gather(
                    [side.at[:, h] for side in sides],
                    slots[a],
                    half,
                    buffer.at[h, a],
                    sems.at[h, a],
                    wait,
                )

        @pl.when(pl.program_id(0) == 0)
        def _():
            for h in range(buffer.shape[0]):
                copies(h, False)

        for h in range(at_once):
            copies(first_head + h, True)
    jobs, places = [], []
    text = text_bias(mask_ref)
    for a in range(2):
        bias = [tile_bias(tile_rows[pos[0] * 2 + a], range(chunks), half, rows, span), text]
        if early:
            bias += others_bias(tile_rows, pos[0], slots[a], range(early), half, rows, span)
        bias = jnp.concatenate(bias, 1)
        own = slice(a * half, (a + 1) * half)
        for h in range(at_once):
            both = []
            for i in range(2):
                pieces = [ref[i, h, own, :] for ref in kv_refs] + [text_ref[i, h]]
                if early:
                    pieces.append(buffer[first_head + h, a, i])
                both.append(jnp.concatenate(pieces, 0))
            query = jnp.concatenate([ref[h, own, :] for ref in q_refs], 0)
            jobs.append((query, both[0], with_ones(both[1]), bias))
            places.append((h, own))
    for (h, own), (highest, blended, total) in zip(places, softmax_parts(jobs)):
        normal = blended / total
        log = highest + jnp.log(total) / LN2
        for c in range(chunks):
            out_ref[h, c, own, :] = normal[c * half : (c + 1) * half]
            log_ref[h, c, own, :] = log[c * half : (c + 1) * half]


def own_attention(pos, tile_rows, pattern, q_list, kv_list, sides, text_kv, mask, parts):
    chunks = len(q_list)
    early = len(sides) // 3
    heads, tokens, _ = q_list[0].shape
    state = jax.ShapeDtypeStruct((heads, chunks, tokens, HD), F32)
    other = 3 * early * tokens // 2
    keys = chunks * tokens // 2 + TEXT + other
    hb = heads_at_once(heads)
    scratch = [
        pltpu.VMEM((heads, 2, 2, other, HD), BF16),
        pltpu.SemaphoreType.DMA((heads, 2, 3, early)),
    ]
    return pl.pallas_call(
        functools.partial(own_kernel, chunks, parts, early),
        out_shape=(state, state),
        grid_spec=pltpu.PrefetchScalarGridSpec(
            num_scalar_prefetch=3,
            grid=(heads // hb,),
            in_specs=[spec((hb, tokens, HD), lambda h, *_: (h, 0, 0))] * chunks
            + [spec((2, hb, tokens, HD), lambda h, *_: (0, h, 0, 0))] * chunks
            + [pl.BlockSpec(memory_space=pl.ANY)] * (3 * early)
            + [
                spec((2, hb, TEXT, HD), lambda h, *_: (0, h, 0, 0)),
                spec((1, TEXT), lambda h, *_: (0, 0), True),
            ],
            out_specs=(spec((hb, chunks, tokens, HD), lambda h, *_: (h, 0, 0, 0)),) * 2,
            scratch_shapes=scratch if early else [],
        ),
        compiler_params=pltpu.CompilerParams(vmem_limit_bytes=VMEM),
        cost_estimate=pl.CostEstimate(
            flops=4 * heads * chunks * tokens * keys * HD,
            bytes_accessed=heads * chunks * tokens * HD * 16,
            transcendentals=heads * chunks * tokens * keys,
        ),
        name="own_attention",
    )(pos, tile_rows, pattern, *q_list, *kv_list, *sides, text_kv, mask)


def tile_kernel(chunks, targets, blocks, parts, pos, tile_rows, pattern, *refs):
    q_refs = refs[:chunks]
    sides = refs[chunks : chunks + 3]
    out_state, log_state = refs[chunks + 3 : chunks + 5]
    outs = refs[chunks + 5 : -2]
    buffer, sems = refs[-2:]
    at_once, half, _ = q_refs[0].shape
    rows = 2 * half // parts
    span = F // parts * H * TW
    band, this = pos[0], pos[1]
    tile = (this ^ targets[0]) * blocks // (parts // 2)
    slots = [pattern[tile, e + 1] for e in range(3)]
    first_head = pl.program_id(0) * at_once

    def copies(h, wait):
        gather([side.at[:, h] for side in sides], slots, half, buffer.at[h], sems.at[h], wait)

    @pl.when(pl.program_id(0) == 0)
    def _():
        for h in range(buffer.shape[0]):
            copies(h, False)

    for h in range(at_once):
        copies(first_head + h, True)
    bias = jnp.concatenate(
        others_bias(tile_rows, band, slots, [chunks - 1], half, rows, span), 1
    )
    jobs, places = [], []
    together = max(JOB // rows, 1)
    for h in range(at_once):
        key = buffer[first_head + h, 0]
        value = with_ones(buffer[first_head + h, 1])
        pieces = []
        for t, k in enumerate(targets):
            for c in range(chunks):
                for i in range(blocks):
                    source = (this ^ k) * blocks + i
                    inner = lax.rem(source, parts // 2)
                    at = pl.ds(pl.multiple_of(inner * rows, 16), rows)
                    pieces.append((h, t, c, i, source, at))
        for low in range(0, len(pieces), together):
            group = pieces[low : low + together]
            query = jnp.concatenate([q_refs[c][h, at, :] for h, _, c, _, _, at in group], 0)
            jobs.append((query, key, value, bias))
            places.append(group)
    real = tile_rows[band * 2 + tile]
    results = (
        (place, [x[n * rows : (n + 1) * rows] for x in found])
        for group, found in zip(places, softmax_parts(jobs))
        for n, place in enumerate(group)
    )
    for (h, t, c, i, source, at), (top, blended, total) in results:
        log = log_state[h, c, at, :]
        most = jnp.maximum(log, top)
        first = jnp.exp2(log - most)
        second = jnp.exp2(top - most)
        result = (out_state[h, c, at, :] * first + blended * second) / (first + total * second)
        place = (
            lax.rem(source, parts // 2) * span
            + c * rows
            + lax.broadcasted_iota(jnp.int32, result.shape, 0)
        )
        low = (c * blocks + i) * rows
        outs[t][low : low + rows, h * HD : (h + 1) * HD] = jnp.where(
            place < real, result, 0.0
        ).astype(BF16)


def tile_attention(pos, tile_rows, pattern, q_list, sides, states, targets, blocks, parts):
    chunks = len(q_list)
    heads, tokens, _ = q_list[0].shape
    rows = tokens // parts * blocks * chunks
    keys = 3 * tokens // 2
    hb = heads_at_once(heads)

    def tile_of(pos_ref):
        return (pos_ref[1] ^ targets[0]) * blocks // (parts // 2)

    return pl.pallas_call(
        functools.partial(tile_kernel, chunks, targets, blocks, parts),
        out_shape=[jax.ShapeDtypeStruct((rows, heads * HD), BF16)] * len(targets),
        grid_spec=pltpu.PrefetchScalarGridSpec(
            num_scalar_prefetch=3,
            grid=(heads // hb,),
            in_specs=[spec((hb, tokens // 2, HD), lambda h, s, *_: (h, tile_of(s), 0))] * chunks
            + [pl.BlockSpec(memory_space=pl.ANY)] * 3
            + [
                spec((hb, chunks, tokens // 2, HD), lambda h, s, *_: (h, 0, tile_of(s), 0))
            ]
            * 2,
            out_specs=[spec((rows, hb * HD), lambda h, *_: (0, h))] * len(targets),
            scratch_shapes=[
                pltpu.VMEM((heads, 2, keys, HD), BF16),
                pltpu.SemaphoreType.DMA((heads, 3, 1)),
            ],
        ),
        compiler_params=pltpu.CompilerParams(vmem_limit_bytes=VMEM),
        cost_estimate=pl.CostEstimate(
            flops=4 * heads * rows * len(targets) * keys * HD,
            bytes_accessed=heads * (keys * HD * 4 + chunks * tokens * HD * 10),
            transcendentals=heads * rows * len(targets) * keys,
        ),
        name="tile_attention",
    )(pos, tile_rows, pattern, *q_list, *sides, *states)


def text_kernel(chunks, parts, pos, tile_rows, *refs):
    kv_refs = refs[:chunks]
    q_ref, text_ref, mask_ref, out_ref = refs[chunks:]
    at_once, tokens, _ = kv_refs[0].shape[1:]
    half = tokens // 2
    rows = tokens // parts
    span = F // parts * H * TW
    first_head = pl.program_id(0) * at_once
    width = out_ref.shape[1] - HD
    own = [
        tile_bias(tile_rows[pos[0] * 2 + a], range(chunks), half, rows, span) for a in range(2)
    ]
    bias = jnp.concatenate(
        [own[a][:, c * half : (c + 1) * half] for c in range(chunks) for a in range(2)]
        + [jnp.where(pos[0] == 0, text_bias(mask_ref), NEG)],
        1,
    )
    size = TEXT
    jobs, places = [], []
    for h in range(at_once):
        key = jnp.concatenate([ref[0, h] for ref in kv_refs] + [text_ref[0, h]], 0)
        value = with_ones(jnp.concatenate([ref[1, h] for ref in kv_refs] + [text_ref[1, h]], 0))
        for low in range(0, TEXT, size):
            jobs.append((q_ref[h, low : low + size, :], key, value, bias))
            places.append((h, slice(low, low + size)))

    @pl.when(pl.program_id(0) == 0)
    def _():
        out_ref[:, width:] = jnp.zeros((TEXT, HD), BF16)

    for (h, mine), (highest, blended, total) in zip(places, softmax_parts(jobs)):
        head = first_head + h
        out_ref[mine, pl.ds(pl.multiple_of(head * HD, HD), HD)] = (blended / total).astype(BF16)
        log = highest + jnp.log(total) / LN2
        lane = lax.broadcasted_iota(jnp.int32, log.shape, 1)
        stats = out_ref[mine, width:].astype(F32)
        for i in range(3):
            term = log.astype(BF16).astype(F32)
            stats = jnp.where(lane == 3 * head + i, term, stats)
            log = log - term
        out_ref[mine, width:] = stats.astype(BF16)


def text_attention(pos, tile_rows, kv_list, text_kv, text_q, mask, parts):
    chunks = len(kv_list)
    _, heads, tokens, _ = kv_list[0].shape
    width = heads * HD
    keys = chunks * tokens + TEXT
    hb = heads_at_once(heads)
    return pl.pallas_call(
        functools.partial(text_kernel, chunks, parts),
        out_shape=jax.ShapeDtypeStruct((TEXT, width + HD), BF16),
        grid_spec=pltpu.PrefetchScalarGridSpec(
            num_scalar_prefetch=2,
            grid=(heads // hb,),
            in_specs=[spec((2, hb, tokens, HD), lambda h, *_: (0, h, 0, 0))] * chunks
            + [
                spec((hb, TEXT, HD), lambda h, *_: (h, 0, 0)),
                spec((2, hb, TEXT, HD), lambda h, *_: (0, h, 0, 0)),
                spec((1, TEXT), lambda h, *_: (0, 0), True),
            ],
            out_specs=spec((TEXT, width + HD), lambda h, *_: (0, 0)),
        ),
        compiler_params=pltpu.CompilerParams(vmem_limit_bytes=VMEM),
        cost_estimate=pl.CostEstimate(
            flops=4 * heads * TEXT * keys * HD,
            bytes_accessed=4 * width * (chunks * tokens + TEXT),
            transcendentals=heads * TEXT * keys,
        ),
        name="text_attention",
    )(pos, tile_rows, *kv_list, text_q, text_kv, mask)


def merge_kernel(*refs):
    parts, out_ref = refs[:-1], refs[-1]
    width = out_ref.shape[1]
    for h in range(width // HD):
        logs = [
            sum(ref[:, width + 3 * h + i : width + 3 * h + i + 1].astype(F32) for i in range(3))
            for ref in parts
        ]
        most = functools.reduce(jnp.maximum, logs)
        factors = [jnp.exp2(log - most) for log in logs]
        column = slice(h * HD, (h + 1) * HD)
        total = sum(factors)
        blended = sum(f * ref[:, column].astype(F32) for f, ref in zip(factors, parts))
        out_ref[:, column] = (blended / total).astype(BF16)


def merge_text(parts):
    rows, wide = parts[0].shape
    return pl.pallas_call(
        merge_kernel,
        out_shape=jax.ShapeDtypeStruct((rows, wide - HD), BF16),
        name="merge_text",
    )(*parts)


def output_kernel(count, layout, pos, *refs):
    latent_refs = refs[:count]
    text_refs = refs[count : 2 * count]
    pieces = refs[2 * count : 2 * count + len(layout)]
    gate_ref, update_ref, text_update_ref, held = refs[2 * count + len(layout) :]
    rows = update_ref.shape[0]

    @pl.when(pl.program_id(0) == 0)
    def _():
        for k in range(count):
            held[k, :rows] = latent_refs[k][...]
            held[k, rows:] = text_refs[k][...]

    terms = {}
    for (k, low, moves, group), w_ref in zip(layout, pieces):
        column = pl.ds(low, w_ref.shape[0])
        if moves:
            column = pl.ds(pl.multiple_of(low + pos[2] * moves, 128), w_ref.shape[0])
        term = jnp.dot(held[k, :, column], w_ref[...], preferred_element_type=F32)
        terms[group] = terms[group] + term if group in terms else term
    total = sum(term.astype(BF16).astype(F32) for term in terms.values())
    result = (total * gate_ref[...]).astype(BF16)
    update_ref[...] = result[:rows]
    text_update_ref[...] = result[rows:]


def output(pos, latent_parts, text_parts, weights, groups, gate):
    count = len(latent_parts)
    rows, width = latent_parts[0].shape
    text_rows = text_parts[0].shape[0]
    block = 512
    layout = [(k, low, moves, groups[k]) for k, low, moves, _ in weights]
    return pl.pallas_call(
        functools.partial(output_kernel, count, layout),
        out_shape=(
            jax.ShapeDtypeStruct((rows, D), BF16),
            jax.ShapeDtypeStruct((text_rows, D), BF16),
        ),
        grid_spec=pltpu.PrefetchScalarGridSpec(
            num_scalar_prefetch=1,
            grid=(D // block,),
            in_specs=[spec((rows, width), lambda j, *_: (0, 0), True)] * count
            + [spec((text_rows, width), lambda j, *_: (0, 0), True)] * count
            + [spec((w.shape[0], block), lambda j, *_: (0, j)) for _, _, _, w in weights]
            + [spec((1, block), lambda j, *_: (0, j))],
            out_specs=(
                spec((rows, block), lambda j, *_: (0, j)),
                spec((text_rows, block), lambda j, *_: (0, j)),
            ),
            scratch_shapes=[pltpu.VMEM((count, rows + text_rows, width), BF16)],
        ),
        compiler_params=pltpu.CompilerParams(vmem_limit_bytes=VMEM),
        cost_estimate=pl.CostEstimate(
            flops=2 * (rows + text_rows) * D * D,
            bytes_accessed=2 * D * (D + 2 * (rows + text_rows)),
            transcendentals=0,
        ),
        name="output",
    )(pos, *latent_parts, *text_parts, *[w for _, _, _, w in weights], gate)


def shards(
    latent,
    text_tokens,
    mod_shift,
    mod_scale,
    mod_gate,
    project_in,
    project_out,
    q_gain,
    k_gain,
    pattern,
    tile_rows,
    text_mask,
):
    heads = lax.axis_size("head")
    bands = lax.axis_size("tile")
    this = lax.axis_index("head")
    band = lax.axis_index("tile")
    width = latent.shape[3]
    frames = latent.shape[0]
    chunks = 2 if frames % 2 == 0 else 1
    step = frames // chunks
    rows = step * H * TW
    tokens = bands * rows
    blocks = F // heads // frames
    assert blocks >= 1 and (blocks == 1 or chunks == 1) and heads & (heads - 1) == 0

    weights = jnp.transpose(project_in, (1, 0, 2))
    mod_shift = mod_shift[None, :]
    mod_scale = mod_scale[None, :]
    q_gain = q_gain[None, :]
    k_gain = k_gain[None, :]
    mask = text_mask[None, :]
    pos = jnp.stack([band, this, lax.axis_index("group")]).astype(jnp.int32)
    norm = (mod_shift, mod_scale, weights, q_gain, k_gain)
    groups = lax.axis_size("group")

    split = groups == 2 and width % 768 == 0
    half_width = width // 2
    pieces = ((0, width // 3), (width // 3, half_width - width // 3)) if split else ((0, width),)
    group = lax.axis_index("group") if split else 0
    own_weights = [
        lax.dynamic_slice_in_dim(project_out, group * half_width + low, size, 0)
        if split
        else project_out
        for low, size in pieces
    ]
    crossed = {}
    for k in range(2, heads, 2):
        for p, piece in enumerate(own_weights):
            crossed[k, p, 0] = lax.ppermute(piece, "head", xor(heads, k))
            if split:
                crossed[k, p, 1] = lax.ppermute(crossed[k, p, 0], "group", xor(2, 1))

    text_kv, text_q = project(
        [text_tokens] * heads,
        [
            spec((TEXT, width), functools.partial(lambda k, c, s: (0, k), k), True)
            for k in range(heads)
        ],
        pos,
        1,
        TEXT,
        True,
        *norm,
    )

    parts = []
    for c in range(chunks):
        own = latent[c * step : (c + 1) * step]

        def piece(s):
            at = lax.rem(band + s, bands) * TW
            return lax.dynamic_slice_in_dim(own, at, TW, 2).reshape(rows, width)

        parts.append(
            [piece(0)]
            + [lax.ppermute(piece(s), "tile", shift(bands, s)) for s in range(1, bands)]
        )
    gathered = []
    for c in range(chunks):
        mine = jnp.concatenate(parts[c], 0)
        received = {0: mine}
        for k in range(2, heads, 2):
            received[k] = lax.ppermute(mine, "head", xor(heads, k))
        for k in range(0, heads, 2):
            received[k + 1] = lax.ppermute(received[k], "head", xor(heads, 1))
        gathered.append([received[k] for k in range(heads)])

    q_list, kv = [], []
    for c in range(chunks):
        kv_part, q_part = project(
            gathered[c],
            [spec((tokens, width), lambda c, s: (0, 0), True)] * heads,
            pos,
            bands,
            rows,
            False,
            *norm,
        )
        q_list.append(q_part)
        kv.append(kv_part)

    forward = [(i, i + 1) for i in range(bands - 1)]
    backward = [(i + 1, i) for i in range(bands - 1)]
    low = [lax.ppermute(part, "tile", forward) for part in kv]
    high = [lax.ppermute(part, "tile", backward) for part in kv]

    share = text_attention(pos, tile_rows, kv, text_kv, text_q, mask, bands)
    count = TEXT // bands

    def text_piece(s):
        return lax.dynamic_slice_in_dim(share, lax.rem(band + s, bands) * count, count, 0)

    text_part = merge_text(
        [text_piece(0)]
        + [lax.ppermute(text_piece(s), "tile", shift(bands, s)) for s in range(1, bands)],
    )
    everyone = [text_part] + [
        lax.ppermute(text_part, "tile", shift(bands, s)) for s in range(1, bands)
    ]
    text_rows = TEXT // heads
    text_parts = []
    for k in range(heads):
        part = jnp.concatenate(
            [
                lax.select_n(
                    lax.rem(band - (this ^ k) * (text_rows // count) - i + bands, bands), *everyone
                )
                for i in range(text_rows // count)
            ],
            0,
        )
        text_parts.append(lax.ppermute(part, "head", xor(heads, k)) if k else part)

    early = [part for side in (low, kv, high) for part in side[:-1]]
    states = own_attention(pos, tile_rows, pattern, q_list, kv, early, text_kv, mask, bands)

    latent_parts = {}
    for far in (1, 0):
        targets = [k for k in range(heads) if k // (heads // 2) == far]
        outs = tile_attention(
            pos,
            tile_rows,
            pattern,
            q_list,
            [low[-1], kv[-1], high[-1]],
            states,
            targets,
            blocks,
            bands,
        )
        for k, part in zip(targets, outs):
            latent_parts[k] = lax.ppermute(part, "head", xor(heads, k)) if k else part

    held = [(0, 0, 0, project_out), (1, 0, 0, lax.ppermute(project_out, "head", xor(heads, 1)))]
    for (k, p, far), value in crossed.items():
        partner = lax.ppermute(value, "head", xor(heads, 1))
        start = pieces[p][0]
        moves = (1 if far == 0 else -1) * half_width if split else 0
        base = half_width if split and far else 0
        held += [(k, base + start, moves, value), (k + 1, base + start, moves, partner)]

    update, text_update = output(
        pos,
        [latent_parts[k] for k in range(heads)],
        text_parts,
        held,
        [k * GROUPS // heads for k in range(heads)],
        mod_gate[None, :],
    )
    return (update.reshape(F // heads, H, TW, D), text_update)


def solution(mesh):
    placed = (
        P(("group", "tile"), None, None, "head"),
        P("group", None),
        P(),
        P(),
        P(),
        P(None, None, "head"),
        P("head", None),
        P(),
        P(),
        P("tile", None),
        P("group"),
        P("group"),
    )
    return jax.shard_map(
        shards,
        mesh=mesh,
        in_specs=placed,
        out_specs=(P(("group", "head"), None, "tile", None), P(("group", "head"), None)),
        check_vma=False,
    )
```

```python
import functools
import math

import jax
import jax.numpy as jnp
from jax import lax
from jax.experimental import pallas as pl
from jax.experimental.pallas import tpu as pltpu
from jax.sharding import PartitionSpec as P

D = 3072
HD = 128
F = 16
H = 6
TW = 8
TEXT = 256
GROUPS = 4
EPSILON = 1e-06
NEG = -1e30
VMEM = 58 << 20
JOB = 384
FACTOR = math.log2(math.e) / math.sqrt(HD)
LN2 = math.log(2.0)
F32 = jnp.float32
BF16 = jnp.bfloat16


def spec(shape, index_map, single=False):
    if single:
        return pl.BlockSpec(shape, index_map, pipeline_mode=pl.Buffered(1))
    return pl.BlockSpec(shape, index_map)


def xor(count, k):
    return [(i, i ^ k) for i in range(count)]


def shift(count, s):
    return [(i, (i + s) % count) for i in range(count)]


def rms(values, gain):
    square = jnp.mean(values * values, axis=-1, keepdims=True)
    return (values * lax.rsqrt(square + EPSILON) * gain).astype(BF16)


def project_kernel(parts, rows, count, ordered, pos, *refs):
    shards = refs[:count]
    shift_ref, scale_ref, weights, q_gain, k_gain, kv_ref, q_ref, normed, held, sems = refs[count:]
    width = shards[0].shape[1]
    step = 16
    block = 256 if width % 256 == 0 else HD
    loads = sems.shape[1]
    deep = D // loads

    def load(c, j):
        low = pl.ds(j * deep, deep)
        return pltpu.make_async_copy(
            weights.at[(c + 1) % 3, low], held.at[c, low], sems.at[c, j]
        )

    for c in range(3):
        for j in range(loads):
            load(c, j).start()

    def norm(i, carry):
        start = pl.multiple_of(i * step, step)
        if parts == 1:
            target = start
        else:
            part = start // rows
            source = lax.rem(pos[0] - part + parts, parts)
            target = pl.multiple_of(source * rows + start - part * rows, step)
        wide = [ref[pl.ds(start, step), :].astype(F32) for ref in shards]
        total = jnp.sum(sum(wide), axis=-1, keepdims=True)
        center = total / D
        offset = [x - center for x in wide]
        variance = jnp.sum(sum(x * x for x in offset), axis=-1, keepdims=True) / D
        inverse = lax.rsqrt(variance + EPSILON)
        for k in range(count):
            owner = k if ordered else pos[1] ^ k
            column = pl.ds(pl.multiple_of(owner * width, 128), width)
            normed[pl.ds(target, step), column] = (
                offset[k] * inverse * (1.0 + scale_ref[:, column]) + shift_ref[:, column]
            ).astype(BF16)
        return carry

    lax.fori_loop(0, parts * rows // step, norm, 0, unroll=4)

    per_block = block // HD
    for c in range(3):
        for j in range(loads):
            load(c, j).wait()
        for j in range(width // block):
            product = jnp.dot(
                normed[...], held[c, :, j * block : (j + 1) * block], preferred_element_type=F32
            )
            for i in range(per_block):
                head = j * per_block + i
                piece = product[:, i * HD : (i + 1) * HD]
                if c == 0:
                    kv_ref[0, head] = rms(piece, k_gain[...])
                elif c == 1:
                    kv_ref[1, head] = piece.astype(BF16)
                else:
                    q_ref[head] = rms(piece, q_gain[...])


def project(shards, shard_specs, pos, parts, rows, ordered, mod_shift, mod_scale, weights, q_gain, k_gain):
    count = len(shards)
    tokens = parts * rows
    width = weights.shape[2]
    heads = width // HD
    whole = lambda c, s: (0, 0)
    return pl.pallas_call(
        functools.partial(project_kernel, parts, rows, count, ordered),
        out_shape=(
            jax.ShapeDtypeStruct((2, heads, tokens, HD), BF16),
            jax.ShapeDtypeStruct((heads, tokens, HD), BF16),
        ),
        grid_spec=pltpu.PrefetchScalarGridSpec(
            num_scalar_prefetch=1,
            grid=(1,),
            in_specs=shard_specs
            + [
                spec((1, D), whole, True),
                spec((1, D), whole, True),
                pl.BlockSpec(memory_space=pl.ANY),
                spec((1, HD), whole, True),
                spec((1, HD), whole, True),
            ],
            out_specs=(
                spec((2, heads, tokens, HD), lambda c, s: (0, 0, 0, 0)),
                spec((heads, tokens, HD), lambda c, s: (0, 0, 0)),
            ),
            scratch_shapes=[
                pltpu.VMEM((tokens, D), BF16),
                pltpu.VMEM((3, D, width), BF16),
                pltpu.SemaphoreType.DMA((3, 4)),
            ],
        ),
        compiler_params=pltpu.CompilerParams(vmem_limit_bytes=VMEM),
        cost_estimate=pl.CostEstimate(
            flops=6 * tokens * D * width,
            bytes_accessed=2 * (2 * tokens * D + 3 * width * (D + tokens)),
            transcendentals=0,
        ),
        name="project",
    )(pos, *shards, mod_shift, mod_scale, weights, q_gain, k_gain)


def scores_of(query, key, bias):
    return (
        lax.dot_general(query, key, (((1,), (1,)), ((), ())), preferred_element_type=F32) + bias
    )


def with_ones(value):
    return jnp.concatenate([value, jnp.ones_like(value)], 1)


def softmax_parts(jobs):
    scores = scores_of(jobs[0][0], jobs[0][1], jobs[0][3])
    for number, (_, _, value, _) in enumerate(jobs):
        ahead = None
        if number + 1 < len(jobs):
            ahead = scores_of(jobs[number + 1][0], jobs[number + 1][1], jobs[number + 1][3])
        highest = jnp.max(scores, axis=-1, keepdims=True)
        weights = jnp.exp2((scores - highest) * FACTOR).astype(BF16)
        both = jnp.dot(weights, value, preferred_element_type=F32)
        yield highest * FACTOR, both[:, :HD], both[:, HD:]
        scores = ahead


def tile_bias(count, chunks, half, rows, span):
    place = lax.broadcasted_iota(jnp.int32, (1, half), 1)
    place = place // rows * span + lax.rem(place, rows)
    return jnp.concatenate(
        [jnp.where(place + c * rows < count, 0.0, NEG) for c in chunks], 1
    )


def text_bias(mask_ref):
    return jnp.where(mask_ref[...] == 1, 0.0, NEG)


def gather(sides, slots, half, buffer, sems, wait):
    count = len(sides) // 3
    for e, slot in enumerate(slots):
        start = pl.multiple_of(lax.rem(slot, 2) * half, half)
        for side in range(3):

            @pl.when(slot // 2 == side)
            def _():
                for c in range(count):
                    copy = pltpu.make_async_copy(
                        sides[side * count + c].at[:, pl.ds(start, half), :],
                        buffer.at[:, pl.ds((e * count + c) * half, half), :],
                        sems.at[e, c],
                    )
                    if wait:
                        copy.wait()
                    else:
                        copy.start()


def others_bias(tile_rows, band, slots, chunks, half, rows, span):
    return [
        tile_bias(
            tile_rows[(band + slot // 2 - 1) * 2 + lax.rem(slot, 2)], chunks, half, rows, span
        )
        for slot in slots
    ]


def heads_at_once(heads):
    return 3 if heads % 3 == 0 else 1


def own_kernel(chunks, parts, early, pos, tile_rows, pattern, *refs):
    q_refs = refs[:chunks]
    kv_refs = refs[chunks : 2 * chunks]
    sides = refs[2 * chunks : 2 * chunks + 3 * early]
    text_ref, mask_ref, out_ref, log_ref = refs[2 * chunks + 3 * early :][:4]
    at_once, tokens, _ = q_refs[0].shape
    half = tokens // 2
    rows = tokens // parts
    span = F // parts * H * TW
    first_head = pl.program_id(0) * at_once
    slots = [[pattern[a, e + 1] for e in range(3)] for a in range(2)]
    if early:
        buffer, sems = refs[-2:]

        def copies(h, wait):
            for a in range(2):
                gather(
                    [side.at[:, h] for side in sides],
                    slots[a],
                    half,
                    buffer.at[h, a],
                    sems.at[h, a],
                    wait,
                )

        @pl.when(pl.program_id(0) == 0)
        def _():
            for h in range(buffer.shape[0]):
                copies(h, False)

        for h in range(at_once):
            copies(first_head + h, True)
    jobs, places = [], []
    text = text_bias(mask_ref)
    for a in range(2):
        bias = [tile_bias(tile_rows[pos[0] * 2 + a], range(chunks), half, rows, span), text]
        if early:
            bias += others_bias(tile_rows, pos[0], slots[a], range(early), half, rows, span)
        bias = jnp.concatenate(bias, 1)
        own = slice(a * half, (a + 1) * half)
        for h in range(at_once):
            both = []
            for i in range(2):
                pieces = [ref[i, h, own, :] for ref in kv_refs] + [text_ref[i, h]]
                if early:
                    pieces.append(buffer[first_head + h, a, i])
                both.append(jnp.concatenate(pieces, 0))
            query = jnp.concatenate([ref[h, own, :] for ref in q_refs], 0)
            jobs.append((query, both[0], with_ones(both[1]), bias))
            places.append((h, own))
    for (h, own), (highest, blended, total) in zip(places, softmax_parts(jobs)):
        normal = blended / total
        log = highest + jnp.log(total) / LN2
        for c in range(chunks):
            out_ref[h, c, own, :] = normal[c * half : (c + 1) * half]
            log_ref[h, c, own, :] = log[c * half : (c + 1) * half]


def own_attention(pos, tile_rows, pattern, q_list, kv_list, sides, text_kv, mask, parts):
    chunks = len(q_list)
    early = len(sides) // 3
    heads, tokens, _ = q_list[0].shape
    state = jax.ShapeDtypeStruct((heads, chunks, tokens, HD), F32)
    other = 3 * early * tokens // 2
    keys = chunks * tokens // 2 + TEXT + other
    hb = heads_at_once(heads)
    scratch = [
        pltpu.VMEM((heads, 2, 2, other, HD), BF16),
        pltpu.SemaphoreType.DMA((heads, 2, 3, early)),
    ]
    return pl.pallas_call(
        functools.partial(own_kernel, chunks, parts, early),
        out_shape=(state, state),
        grid_spec=pltpu.PrefetchScalarGridSpec(
            num_scalar_prefetch=3,
            grid=(heads // hb,),
            in_specs=[spec((hb, tokens, HD), lambda h, *_: (h, 0, 0))] * chunks
            + [spec((2, hb, tokens, HD), lambda h, *_: (0, h, 0, 0))] * chunks
            + [pl.BlockSpec(memory_space=pl.ANY)] * (3 * early)
            + [
                spec((2, hb, TEXT, HD), lambda h, *_: (0, h, 0, 0)),
                spec((1, TEXT), lambda h, *_: (0, 0), True),
            ],
            out_specs=(spec((hb, chunks, tokens, HD), lambda h, *_: (h, 0, 0, 0)),) * 2,
            scratch_shapes=scratch if early else [],
        ),
        compiler_params=pltpu.CompilerParams(vmem_limit_bytes=VMEM),
        cost_estimate=pl.CostEstimate(
            flops=4 * heads * chunks * tokens * keys * HD,
            bytes_accessed=heads * chunks * tokens * HD * 16,
            transcendentals=heads * chunks * tokens * keys,
        ),
        name="own_attention",
    )(pos, tile_rows, pattern, *q_list, *kv_list, *sides, text_kv, mask)


def tile_kernel(chunks, targets, blocks, parts, pos, tile_rows, pattern, *refs):
    q_refs = refs[:chunks]
    sides = refs[chunks : chunks + 3]
    out_state, log_state = refs[chunks + 3 : chunks + 5]
    outs = refs[chunks + 5 : -2]
    buffer, sems = refs[-2:]
    at_once, half, _ = q_refs[0].shape
    rows = 2 * half // parts
    span = F // parts * H * TW
    band, this = pos[0], pos[1]
    tile = (this ^ targets[0]) * blocks // (parts // 2)
    slots = [pattern[tile, e + 1] for e in range(3)]
    first_head = pl.program_id(0) * at_once

    def copies(h, wait):
        gather([side.at[:, h] for side in sides], slots, half, buffer.at[h], sems.at[h], wait)

    @pl.when(pl.program_id(0) == 0)
    def _():
        for h in range(buffer.shape[0]):
            copies(h, False)

    for h in range(at_once):
        copies(first_head + h, True)
    bias = jnp.concatenate(
        others_bias(tile_rows, band, slots, [chunks - 1], half, rows, span), 1
    )
    jobs, places = [], []
    together = max(JOB // rows, 1)
    for h in range(at_once):
        key = buffer[first_head + h, 0]
        value = with_ones(buffer[first_head + h, 1])
        pieces = []
        for t, k in enumerate(targets):
            for c in range(chunks):
                for i in range(blocks):
                    source = (this ^ k) * blocks + i
                    inner = lax.rem(source, parts // 2)
                    at = pl.ds(pl.multiple_of(inner * rows, 16), rows)
                    pieces.append((h, t, c, i, source, at))
        for low in range(0, len(pieces), together):
            group = pieces[low : low + together]
            query = jnp.concatenate([q_refs[c][h, at, :] for h, _, c, _, _, at in group], 0)
            jobs.append((query, key, value, bias))
            places.append(group)
    real = tile_rows[band * 2 + tile]
    results = (
        (place, [x[n * rows : (n + 1) * rows] for x in found])
        for group, found in zip(places, softmax_parts(jobs))
        for n, place in enumerate(group)
    )
    for (h, t, c, i, source, at), (top, blended, total) in results:
        log = log_state[h, c, at, :]
        most = jnp.maximum(log, top)
        first = jnp.exp2(log - most)
        second = jnp.exp2(top - most)
        result = (out_state[h, c, at, :] * first + blended * second) / (first + total * second)
        place = (
            lax.rem(source, parts // 2) * span
            + c * rows
            + lax.broadcasted_iota(jnp.int32, result.shape, 0)
        )
        low = (c * blocks + i) * rows
        outs[t][low : low + rows, h * HD : (h + 1) * HD] = jnp.where(
            place < real, result, 0.0
        ).astype(BF16)


def tile_attention(pos, tile_rows, pattern, q_list, sides, states, targets, blocks, parts):
    chunks = len(q_list)
    heads, tokens, _ = q_list[0].shape
    rows = tokens // parts * blocks * chunks
    keys = 3 * tokens // 2
    hb = heads_at_once(heads)

    def tile_of(pos_ref):
        return (pos_ref[1] ^ targets[0]) * blocks // (parts // 2)

    return pl.pallas_call(
        functools.partial(tile_kernel, chunks, targets, blocks, parts),
        out_shape=[jax.ShapeDtypeStruct((rows, heads * HD), BF16)] * len(targets),
        grid_spec=pltpu.PrefetchScalarGridSpec(
            num_scalar_prefetch=3,
            grid=(heads // hb,),
            in_specs=[spec((hb, tokens // 2, HD), lambda h, s, *_: (h, tile_of(s), 0))] * chunks
            + [pl.BlockSpec(memory_space=pl.ANY)] * 3
            + [
                spec((hb, chunks, tokens // 2, HD), lambda h, s, *_: (h, 0, tile_of(s), 0))
            ]
            * 2,
            out_specs=[spec((rows, hb * HD), lambda h, *_: (0, h))] * len(targets),
            scratch_shapes=[
                pltpu.VMEM((heads, 2, keys, HD), BF16),
                pltpu.SemaphoreType.DMA((heads, 3, 1)),
            ],
        ),
        compiler_params=pltpu.CompilerParams(vmem_limit_bytes=VMEM),
        cost_estimate=pl.CostEstimate(
            flops=4 * heads * rows * len(targets) * keys * HD,
            bytes_accessed=heads * (keys * HD * 4 + chunks * tokens * HD * 10),
            transcendentals=heads * rows * len(targets) * keys,
        ),
        name="tile_attention",
    )(pos, tile_rows, pattern, *q_list, *sides, *states)


def text_kernel(chunks, parts, pos, tile_rows, *refs):
    kv_refs = refs[:chunks]
    q_ref, text_ref, mask_ref, out_ref = refs[chunks:]
    at_once, tokens, _ = kv_refs[0].shape[1:]
    half = tokens // 2
    rows = tokens // parts
    span = F // parts * H * TW
    first_head = pl.program_id(0) * at_once
    width = out_ref.shape[1] - HD
    own = [
        tile_bias(tile_rows[pos[0] * 2 + a], range(chunks), half, rows, span) for a in range(2)
    ]
    bias = jnp.concatenate(
        [own[a][:, c * half : (c + 1) * half] for c in range(chunks) for a in range(2)]
        + [jnp.where(pos[0] == 0, text_bias(mask_ref), NEG)],
        1,
    )
    size = TEXT
    jobs, places = [], []
    for h in range(at_once):
        key = jnp.concatenate([ref[0, h] for ref in kv_refs] + [text_ref[0, h]], 0)
        value = with_ones(jnp.concatenate([ref[1, h] for ref in kv_refs] + [text_ref[1, h]], 0))
        for low in range(0, TEXT, size):
            jobs.append((q_ref[h, low : low + size, :], key, value, bias))
            places.append((h, slice(low, low + size)))

    @pl.when(pl.program_id(0) == 0)
    def _():
        out_ref[:, width:] = jnp.zeros((TEXT, HD), BF16)

    for (h, mine), (highest, blended, total) in zip(places, softmax_parts(jobs)):
        head = first_head + h
        out_ref[mine, pl.ds(pl.multiple_of(head * HD, HD), HD)] = (blended / total).astype(BF16)
        log = highest + jnp.log(total) / LN2
        lane = lax.broadcasted_iota(jnp.int32, log.shape, 1)
        stats = out_ref[mine, width:].astype(F32)
        for i in range(3):
            term = log.astype(BF16).astype(F32)
            stats = jnp.where(lane == 3 * head + i, term, stats)
            log = log - term
        out_ref[mine, width:] = stats.astype(BF16)


def text_attention(pos, tile_rows, kv_list, text_kv, text_q, mask, parts):
    chunks = len(kv_list)
    _, heads, tokens, _ = kv_list[0].shape
    width = heads * HD
    keys = chunks * tokens + TEXT
    hb = heads_at_once(heads)
    return pl.pallas_call(
        functools.partial(text_kernel, chunks, parts),
        out_shape=jax.ShapeDtypeStruct((TEXT, width + HD), BF16),
        grid_spec=pltpu.PrefetchScalarGridSpec(
            num_scalar_prefetch=2,
            grid=(heads // hb,),
            in_specs=[spec((2, hb, tokens, HD), lambda h, *_: (0, h, 0, 0))] * chunks
            + [
                spec((hb, TEXT, HD), lambda h, *_: (h, 0, 0)),
                spec((2, hb, TEXT, HD), lambda h, *_: (0, h, 0, 0)),
                spec((1, TEXT), lambda h, *_: (0, 0), True),
            ],
            out_specs=spec((TEXT, width + HD), lambda h, *_: (0, 0)),
        ),
        compiler_params=pltpu.CompilerParams(vmem_limit_bytes=VMEM),
        cost_estimate=pl.CostEstimate(
            flops=4 * heads * TEXT * keys * HD,
            bytes_accessed=4 * width * (chunks * tokens + TEXT),
            transcendentals=heads * TEXT * keys,
        ),
        name="text_attention",
    )(pos, tile_rows, *kv_list, text_q, text_kv, mask)


def merge_kernel(*refs):
    parts, out_ref = refs[:-1], refs[-1]
    width = out_ref.shape[2]
    for h in range(width // HD):
        logs = [
            sum(ref[:, :, width + 3 * h + i : width + 3 * h + i + 1].astype(F32) for i in range(3))
            for ref in parts
        ]
        most = functools.reduce(jnp.maximum, logs)
        factors = [jnp.exp2(log - most) for log in logs]
        column = slice(h * HD, (h + 1) * HD)
        total = sum(factors)
        blended = sum(f * ref[:, :, column].astype(F32) for f, ref in zip(factors, parts))
        out_ref[:, :, column] = (blended / total).astype(BF16)


def merge_text(parts):
    heads, rows, wide = parts[0].shape
    return pl.pallas_call(
        merge_kernel,
        out_shape=jax.ShapeDtypeStruct((heads, rows, wide - HD), BF16),
        name="merge_text",
    )(*parts)


def output_kernel(count, shares, layout, pos, *refs):
    latent_refs = refs[:count]
    text_refs = refs[count : count + shares]
    pieces = refs[count + shares : count + shares + len(layout)]
    gate_ref, update_ref, text_update_ref, held, weights, total, sems = refs[
        count + shares + len(layout) :
    ]
    rows = update_ref.shape[0]
    width = held.shape[2]
    block = 512

    copies = []
    for n, ((k, low, moves, group), ref) in enumerate(zip(layout, pieces)):
        start = k * width + low
        if moves:
            start = pl.multiple_of(start + pos[2] * moves, 128)
        copy = pltpu.make_async_copy(ref, weights.at[pl.ds(start, ref.shape[0])], sems.at[n])
        copy.start()
        copies.append((group, copy))

    for k in range(count):
        held[k, :rows] = latent_refs[k][...]
        for s, ref in enumerate(text_refs):
            size = ref.shape[1]
            low = rows
            if shares > 1:
                low = pl.multiple_of(rows + lax.rem(pos[0] - s + shares, shares) * size, 16)
            held[k, pl.ds(low, size)] = ref[k]

    groups = sorted({group for group, _ in copies})
    for group in groups:
        for other, copy in copies:
            if other == group:
                copy.wait()
        members = sorted({k for k, _, _, other in layout if other == group})
        for low in range(0, D, block):
            column = slice(low, low + block)
            term = sum(
                jnp.dot(
                    held[k],
                    weights[k * width : (k + 1) * width, column],
                    preferred_element_type=F32,
                )
                for k in members
            )
            term = term.astype(BF16).astype(F32)
            if group != groups[0]:
                term = total[:, column] + term
            if group != groups[-1]:
                total[:, column] = term
            else:
                result = (term * gate_ref[:, column]).astype(BF16)
                update_ref[:, column] = result[:rows]
                text_update_ref[:, column] = result[rows:]


def output(pos, latent_parts, text_shares, weights, groups, gate):
    count = len(latent_parts)
    shares = len(text_shares)
    rows, width = latent_parts[0].shape
    text_rows = text_shares[0].shape[1] * shares
    layout = [(k, low, moves, groups[k]) for k, low, moves, _ in weights]
    return pl.pallas_call(
        functools.partial(output_kernel, count, shares, layout),
        out_shape=(
            jax.ShapeDtypeStruct((rows, D), BF16),
            jax.ShapeDtypeStruct((text_rows, D), BF16),
        ),
        grid_spec=pltpu.PrefetchScalarGridSpec(
            num_scalar_prefetch=1,
            grid=(1,),
            in_specs=[spec((rows, width), lambda j, *_: (0, 0), True)] * count
            + [spec(text_shares[0].shape, lambda j, *_: (0, 0, 0), True)] * shares
            + [pl.BlockSpec(memory_space=pl.ANY)] * len(weights)
            + [spec((1, D), lambda j, *_: (0, 0), True)],
            out_specs=(
                spec((rows, D), lambda j, *_: (0, 0), True),
                spec((text_rows, D), lambda j, *_: (0, 0), True),
            ),
            scratch_shapes=[
                pltpu.VMEM((count, rows + text_rows, width), BF16),
                pltpu.VMEM((D, D), BF16),
                pltpu.VMEM((rows + text_rows, D), F32),
                pltpu.SemaphoreType.DMA((len(weights),)),
            ],
        ),
        compiler_params=pltpu.CompilerParams(vmem_limit_bytes=VMEM),
        cost_estimate=pl.CostEstimate(
            flops=2 * (rows + text_rows) * D * D,
            bytes_accessed=2 * D * (D + 2 * (rows + text_rows)),
            transcendentals=0,
        ),
        name="output",
    )(pos, *latent_parts, *text_shares, *[w for _, _, _, w in weights], gate)


def shards(
    latent,
    text_tokens,
    mod_shift,
    mod_scale,
    mod_gate,
    project_in,
    project_out,
    q_gain,
    k_gain,
    pattern,
    tile_rows,
    text_mask,
):
    heads = lax.axis_size("head")
    bands = lax.axis_size("tile")
    this = lax.axis_index("head")
    band = lax.axis_index("tile")
    width = latent.shape[3]
    frames = latent.shape[0]
    chunks = 2 if frames % 2 == 0 else 1
    step = frames // chunks
    rows = step * H * TW
    tokens = bands * rows
    blocks = F // heads // frames
    assert blocks >= 1 and (blocks == 1 or chunks == 1) and heads & (heads - 1) == 0

    weights = jnp.transpose(project_in, (1, 0, 2))
    mod_shift = mod_shift[None, :]
    mod_scale = mod_scale[None, :]
    q_gain = q_gain[None, :]
    k_gain = k_gain[None, :]
    mask = text_mask[None, :]
    pos = jnp.stack([band, this, lax.axis_index("group")]).astype(jnp.int32)
    norm = (mod_shift, mod_scale, weights, q_gain, k_gain)
    groups = lax.axis_size("group")

    split = groups == 2 and width % 768 == 0
    half_width = width // 2
    pieces = ((0, width // 3), (width // 3, half_width - width // 3)) if split else ((0, width),)
    group = lax.axis_index("group") if split else 0
    own_weights = [
        lax.dynamic_slice_in_dim(project_out, group * half_width + low, size, 0)
        if split
        else project_out
        for low, size in pieces
    ]
    crossed = {}
    for k in range(2, heads, 2):
        for p, piece in enumerate(own_weights):
            crossed[k, p, 0] = lax.ppermute(piece, "head", xor(heads, k))
            if split:
                crossed[k, p, 1] = lax.ppermute(crossed[k, p, 0], "group", xor(2, 1))

    text_kv, text_q = project(
        [text_tokens] * heads,
        [
            spec((TEXT, width), functools.partial(lambda k, c, s: (0, k), k), True)
            for k in range(heads)
        ],
        pos,
        1,
        TEXT,
        True,
        *norm,
    )

    parts = []
    for c in range(chunks):
        own = latent[c * step : (c + 1) * step]

        def piece(s):
            at = lax.rem(band + s, bands) * TW
            return lax.dynamic_slice_in_dim(own, at, TW, 2).reshape(rows, width)

        parts.append(
            [piece(0)]
            + [lax.ppermute(piece(s), "tile", shift(bands, s)) for s in range(1, bands)]
        )
    gathered = []
    for c in range(chunks):
        mine = jnp.concatenate(parts[c], 0)
        received = {0: mine}
        for k in range(2, heads, 2):
            received[k] = lax.ppermute(mine, "head", xor(heads, k))
        for k in range(0, heads, 2):
            received[k + 1] = lax.ppermute(received[k], "head", xor(heads, 1))
        gathered.append([received[k] for k in range(heads)])

    q_list, kv = [], []
    for c in range(chunks):
        kv_part, q_part = project(
            gathered[c],
            [spec((tokens, width), lambda c, s: (0, 0), True)] * heads,
            pos,
            bands,
            rows,
            False,
            *norm,
        )
        q_list.append(q_part)
        kv.append(kv_part)

    forward = [(i, i + 1) for i in range(bands - 1)]
    backward = [(i + 1, i) for i in range(bands - 1)]
    low = [lax.ppermute(part, "tile", forward) for part in kv]
    high = [lax.ppermute(part, "tile", backward) for part in kv]

    share = text_attention(pos, tile_rows, kv, text_kv, text_q, mask, bands)
    text_rows = TEXT // heads
    count = text_rows // bands
    shared = []
    for k in range(heads):
        part = lax.dynamic_slice_in_dim(share, (this ^ k) * text_rows, text_rows, 0)
        shared.append(lax.ppermute(part, "head", xor(heads, k)) if k else part)
    shared = jnp.stack(shared)

    def text_piece(s):
        return lax.dynamic_slice_in_dim(shared, lax.rem(band + s, bands) * count, count, 1)

    text_part = merge_text(
        [text_piece(0)]
        + [lax.ppermute(text_piece(s), "tile", shift(bands, s)) for s in range(1, bands)],
    )
    text_shares = [text_part] + [
        lax.ppermute(text_part, "tile", shift(bands, s)) for s in range(1, bands)
    ]
    if count % 16:
        text_shares = [
            jnp.concatenate(
                [lax.select_n(lax.rem(band - i + bands, bands), *text_shares) for i in range(bands)],
                1,
            )
        ]

    early = [part for side in (low, kv, high) for part in side[:-1]]
    states = own_attention(pos, tile_rows, pattern, q_list, kv, early, text_kv, mask, bands)

    latent_parts = {}
    for far in (1, 0):
        targets = [k for k in range(heads) if k // (heads // 2) == far]
        outs = tile_attention(
            pos,
            tile_rows,
            pattern,
            q_list,
            [low[-1], kv[-1], high[-1]],
            states,
            targets,
            blocks,
            bands,
        )
        for k, part in zip(targets, outs):
            latent_parts[k] = lax.ppermute(part, "head", xor(heads, k)) if k else part

    held = [(0, 0, 0, project_out), (1, 0, 0, lax.ppermute(project_out, "head", xor(heads, 1)))]
    for (k, p, far), value in crossed.items():
        partner = lax.ppermute(value, "head", xor(heads, 1))
        start = pieces[p][0]
        moves = (1 if far == 0 else -1) * half_width if split else 0
        base = half_width if split and far else 0
        held += [(k, base + start, moves, value), (k + 1, base + start, moves, partner)]

    update, text_update = output(
        pos,
        [latent_parts[k] for k in range(heads)],
        text_shares,
        held,
        [k * GROUPS // heads for k in range(heads)],
        mod_gate[None, :],
    )
    return (update.reshape(F // heads, H, TW, D), text_update)


def solution(mesh):
    placed = (
        P(("group", "tile"), None, None, "head"),
        P("group", None),
        P(),
        P(),
        P(),
        P(None, None, "head"),
        P("head", None),
        P(),
        P(),
        P("tile", None),
        P("group"),
        P("group"),
    )
    return jax.shard_map(
        shards,
        mesh=mesh,
        in_specs=placed,
        out_specs=(P(("group", "head"), None, "tile", None), P(("group", "head"), None)),
        check_vma=False,
    )
```
